512 devices in a mesh: section: 4 (over y_lo), video: 8 (over y_hi, x), dp: 16 (over z, core).
Axes of the slice: x: 4, y: 8 (y_hi: 2, y_lo: 4; y = y_hi * 4 + y_lo), z: 8, core: 2. Of those that a mesh axis runs over, the one named last changes fastest.
Arguments:
- grad_latent: bfloat16 [16, 8, 64, 64, 128], P('dp', 'video', 'section'), may hold values from -6 to 6
- input_one: bfloat16 [16, 8, 64, 64, 128], P('dp', 'video', 'section'), may hold values from -6 to 6
- preact_one: bfloat16 [16, 8, 64, 64, 128], P('dp', 'video', 'section'), may hold values from -8 to 8
- input_two: bfloat16 [16, 8, 64, 64, 128], P('dp', 'video', 'section'), may hold values from -6 to 6
- preact_two: bfloat16 [16, 8, 64, 64, 128], P('dp', 'video', 'section'), may hold values from -8 to 8
- spatial_one: bfloat16 [3, 3, 128, 128], replicated, may hold values from -0.1875 to 0.1875
- temporal_one: bfloat16 [3, 128, 128], replicated, may hold values from -0.3125 to 0.3125
- spatial_two: bfloat16 [3, 3, 128, 128], replicated, may hold values from -0.1875 to 0.1875
- temporal_two: bfloat16 [3, 128, 128], replicated, may hold values from -0.3125 to 0.3125
Outputs:
- grad_input: bfloat16 [16, 8, 64, 64, 128], P('dp', 'video', 'section')
- grad_spatial_one: float32 [3, 3, 128, 128], replicated
- grad_temporal_one: float32 [3, 128, 128], replicated
- grad_spatial_two: float32 [3, 3, 128, 128], replicated
- grad_temporal_two: float32 [3, 128, 128], replicated
The draws below stay inside these ranges and needn't reach their ends.
All inputs are finite; a program needn't handle non-finite values.
Results may differ from the reference program's by a relative error of at most 0.0061.
Values may be sent and summed in bfloat16 or wider, within the bound.
A program may use at most 64 MiB of HBM per device.

```python
import jax
import jax.numpy as jnp
from jax import lax

CH = 128
COLS = 64
FRAMES = 8
ROWS = 64
CLIPS = 16


def levels(key, extent, cuts, smallest, largest):
    def one(position, blocks):
        steps = jax.random.uniform(jax.random.fold_in(jax.random.fold_in(key, 6), position), (blocks,), jnp.float32, smallest / len(cuts), largest / len(cuts))
        return jnp.repeat(jnp.exp(steps), extent[position] // blocks).reshape((-1,) + (1,) * (len(extent) - position - 1))

    gain = one(*cuts[0])
    for cut in cuts[1:]:
        gain = gain * one(*cut)
    return gain


def centred(key, shape, spread, most, shards=(), held_as=jnp.bfloat16):
    entries = jax.random.normal(key, shape, jnp.float32) * spread
    if len(shards) > 0:
        entries = levels(key, shape, shards, -0.22, 0.18) * entries
    return jnp.clip(entries, min=-most, max=most).astype(held_as)


def setup_inputs(seed: int = 0) -> dict:
    key_of = jax.random.split(jax.random.key(seed), 10)
    return {
        "grad_latent": centred(key_of[0], (CLIPS, FRAMES, ROWS, COLS, CH), 1.0, 6.0, ((0, 16), (1, 8), (2, 4))),
        "input_one": centred(key_of[1], (CLIPS, FRAMES, ROWS, COLS, CH), 1.0, 6.0, ((0, 16), (1, 8), (2, 4))),
        "preact_one": centred(key_of[2], (CLIPS, FRAMES, ROWS, COLS, CH), 2.0, 8.0, ((0, 16), (1, 8), (2, 4))),
        "input_two": centred(key_of[3], (CLIPS, FRAMES, ROWS, COLS, CH), 1.0, 6.0, ((0, 16), (1, 8), (2, 4))),
        "preact_two": centred(key_of[4], (CLIPS, FRAMES, ROWS, COLS, CH), 2.0, 8.0, ((0, 16), (1, 8), (2, 4))),
        "spatial_one": centred(key_of[5], (3, 3, CH, CH), (9 * CH) ** -0.5, 0.1875),
        "temporal_one": centred(key_of[6], (3, CH, CH), (3 * CH) ** -0.5, 0.3125),
        "spatial_two": centred(key_of[7], (3, 3, CH, CH), (9 * CH) ** -0.5, 0.1875),
        "temporal_two": centred(key_of[8], (3, CH, CH), (3 * CH) ** -0.5, 0.3125),
    }


def spatial_conv(field, kernel):
    return lax.conv_general_dilated(field, kernel, (1, 1), 'SAME', dimension_numbers=('NHWC', 'HWIO', 'NHWC'), precision=lax.Precision.HIGHEST)

def temporal_back(grad_out, act, kernel):
    frames = grad_out.shape[0]
    gz = grad_out.astype(jnp.float32)
    av = act.astype(jnp.float32)
    kf = kernel.astype(jnp.float32)
    gpad = jnp.pad(gz, ((0, 2), (0, 0), (0, 0), (0, 0)))
    apad = jnp.pad(av, ((2, 0), (0, 0), (0, 0), (0, 0)))
    gact = jnp.zeros(gz.shape, jnp.float32)
    kgrads = []
    for k in range(3):
        gact = gact + jnp.einsum('thwo,io->thwi', gpad[2 - k:2 - k + frames], kf[k], precision=lax.Precision.HIGHEST)
        kgrads.append(jnp.einsum('thwi,thwo->io', apad[k:k + frames], gz, precision=lax.Precision.HIGHEST))
    return (gact.astype(jnp.bfloat16), jnp.stack(kgrads))

def block_back(grad_out, saved_in, preact, spatial, temporal):
    hval = preact.astype(jnp.float32)
    sig = jax.nn.sigmoid(hval)
    act = (hval * sig).astype(jnp.bfloat16)
    gact, kgrad_t = temporal_back(grad_out, act, temporal)
    gpre = (gact.astype(jnp.float32) * sig * (1.0 + hval * (1.0 - sig))).astype(jnp.bfloat16)
    _, pullback = jax.vjp(spatial_conv, saved_in.astype(jnp.float32), spatial.astype(jnp.float32))
    gin, kgrad_s = pullback(gpre.astype(jnp.float32))
    grad_in = (grad_out.astype(jnp.float32) + gin).astype(jnp.bfloat16)
    return (grad_in, kgrad_s, kgrad_t)

def one_clip(items, spatial_one, temporal_one, spatial_two, temporal_two):
    grad_latent, input_one, preact_one, input_two, preact_two = items
    grad_mid, gs2, gt2 = block_back(grad_latent, input_two, preact_two, spatial_two, temporal_two)
    grad_in, gs1, gt1 = block_back(grad_mid, input_one, preact_one, spatial_one, temporal_one)
    return (grad_in, gs1, gt1, gs2, gt2)

def reference(grad_latent, input_one, preact_one, input_two, preact_two, spatial_one, temporal_one, spatial_two, temporal_two):

    def step(items):
        return one_clip(items, spatial_one, temporal_one, spatial_two, temporal_two)
    grad_in, gs1, gt1, gs2, gt2 = lax.map(step, (grad_latent, input_one, preact_one, input_two, preact_two))
    scale = 1.0 / jnp.sqrt(jnp.float32(CLIPS * FRAMES * ROWS * COLS))
    return (grad_in, scale * lax.optimization_barrier(jnp.sum(gs1, axis=0)), scale * lax.optimization_barrier(jnp.sum(gt1, axis=0)), scale * lax.optimization_barrier(jnp.sum(gs2, axis=0)), scale * lax.optimization_barrier(jnp.sum(gt2, axis=0)))
```

```python
import functools
import math

import jax
import jax.numpy as jnp
from jax import lax
from jax.experimental import pallas as pl
from jax.experimental.pallas import tpu as pltpu
from jax.sharding import PartitionSpec as P

MESH = pl.DeviceIdType.MESH
F32 = jnp.float32
BF16 = jnp.bfloat16
XS = 4
CORES = 2


class Place:
    def __init__(self, sizes):
        self.S, self.V, self.D = sizes
        self.X = min(XS, self.V)
        self.YH = self.V // self.X
        self.Z = self.D // CORES
        self.n = {"x": self.X, "y": self.YH * self.S, "z": self.Z}
        self.s = lax.axis_index("section")
        self.v = lax.axis_index("video")
        self.d = lax.axis_index("dp")
        self.x = lax.rem(self.v, self.X)
        self.yh = lax.div(self.v, self.X)
        self.z = lax.div(self.d, CORES)
        self.c = lax.rem(self.d, CORES)
        self.at = {"x": self.x, "y": self.yh * self.S + self.s, "z": self.z}

    def peer(self, axis, i):
        if axis == "x":
            return {"video": self.yh * self.X + i}
        if axis == "y":
            return {"section": lax.rem(i, self.S), "video": lax.div(i, self.S) * self.X + self.x}
        return {"dp": i * CORES + self.c}

    def mate(self):
        return {"dp": self.z * CORES + (1 - self.c)}


def remote(src, dst, send, recv, to):
    return pltpu.make_async_remote_copy(
        src_ref=src, dst_ref=dst, send_sem=send, recv_sem=recv, device_id=to, device_id_type=MESH
    )


class Reduce:
    def __init__(self, place, order, scale, refs):
        self.p = place
        self.A, self.B, self.C = order
        self.nA, self.nB, self.nC = (place.n[k] for k in order)
        self.iA, self.iB, self.iC = (place.at[k] for k in order)
        self.scale = scale
        (self.part, self.rcore, self.s0, self.ra, self.s1, self.rb, self.rc, self.out,
         self.ms, self.mr, self.as_, self.ar, self.bs, self.br, self.cs, self.cr,
         self.gbs, self.gbr, self.gas, self.gar) = refs
        self.half = self.nA * self.nB

    def core_send(self):
        p = self.p
        self.m0 = remote(self.part.at[pl.ds((1 - p.c) * self.half, self.half)], self.rcore,
                         self.ms.at[0], self.mr.at[0], p.mate())
        self.m0.start()

    def a_send(self):
        p = self.p
        self.m0.wait_recv()
        self.s0[...] = self.part[pl.ds(p.c * self.half, self.half)] + self.rcore[...]
        for off in range(1, self.nA):
            to = lax.rem(self.iA + off, self.nA)
            remote(self.s0.at[pl.ds(to * self.nB, self.nB)], self.ra.at[self.iA],
                   self.as_.at[to], self.ar.at[self.iA], p.peer(self.A, to)).start()

    def b_send(self):
        p = self.p
        total = self.s0[pl.ds(self.iA * self.nB, self.nB)]
        for off in range(1, self.nA):
            frm = lax.rem(self.iA + off, self.nA)
            remote(self.ra.at[frm], self.ra.at[frm], self.as_.at[frm], self.ar.at[frm], p.peer(self.A, frm)).wait_recv()
            total = total + self.ra[frm]
        self.s1[...] = total
        for off in range(1, self.nB):
            to = lax.rem(self.iB + off, self.nB)
            remote(self.s1.at[to], self.rb.at[self.iB], self.bs.at[to], self.br.at[self.iB], p.peer(self.B, to)).start()

    def c_send(self):
        p = self.p
        total = self.s1[self.iB]
        for off in range(1, self.nB):
            frm = lax.rem(self.iB + off, self.nB)
            remote(self.rb.at[frm], self.rb.at[frm], self.bs.at[frm], self.br.at[frm], p.peer(self.B, frm)).wait_recv()
            total = total + self.rb[frm]
        self.rc[self.iC] = total
        for off in range(1, self.nC):
            to = lax.rem(self.iC + off, self.nC)
            remote(self.rc.at[self.iC], self.rc.at[self.iC], self.cs.at[to], self.cr.at[self.iC], p.peer(self.C, to)).start()

    def row(self, b):
        return pl.ds((self.p.c * self.nA + self.iA) * self.nB + b, 1)

    def col(self, a):
        return pl.ds((self.p.c * self.nA + a) * self.nB, self.nB)

    def gb_send(self):
        p = self.p
        for off in range(1, self.nC):
            frm = lax.rem(self.iC + off, self.nC)
            remote(self.rc.at[frm], self.rc.at[frm], self.cs.at[frm], self.cr.at[frm], p.peer(self.C, frm)).wait_recv()
        total = self.rc[0]
        for i in range(1, self.nC):
            total = total + self.rc[i]
        mine = self.out.at[self.row(self.iB)]
        mine[...] = (total * self.scale)[None]
        for off in range(1, self.nB):
            to = lax.rem(self.iB + off, self.nB)
            remote(mine, mine, self.gbs.at[to], self.gbr.at[self.iB], p.peer(self.B, to)).start()

    def ga_send(self):
        p = self.p
        for off in range(1, self.nB):
            frm = lax.rem(self.iB + off, self.nB)
            there = self.out.at[self.row(frm)]
            remote(there, there, self.gbs.at[frm], self.gbr.at[frm], p.peer(self.B, frm)).wait_recv()
        mine = self.out.at[self.col(self.iA)]
        for off in range(1, self.nA):
            to = lax.rem(self.iA + off, self.nA)
            remote(mine, mine, self.gas.at[to], self.gar.at[self.iA], p.peer(self.A, to)).start()

    def core_gather(self):
        p = self.p
        for off in range(1, self.nA):
            frm = lax.rem(self.iA + off, self.nA)
            there = self.out.at[self.col(frm)]
            remote(there, there, self.gas.at[frm], self.gar.at[frm], p.peer(self.A, frm)).wait_recv()
        mine = self.out.at[pl.ds(p.c * self.half, self.half)]
        self.m1 = remote(mine, mine, self.ms.at[1], self.mr.at[1], p.mate())
        self.m1.start()

    def finish(self):
        p = self.p
        there = self.out.at[pl.ds((1 - p.c) * self.half, self.half)]
        remote(there, there, self.ms.at[1], self.mr.at[1], p.mate()).wait_recv()

    def drain(self):
        p = self.p
        self.m0.wait_send()
        self.m1.wait_send()
        for off in range(1, self.nA):
            to = lax.rem(self.iA + off, self.nA)
            remote(self.s0.at[pl.ds(to * self.nB, self.nB)], self.ra.at[self.iA],
                   self.as_.at[to], self.ar.at[self.iA], p.peer(self.A, to)).wait_send()
            mine = self.out.at[self.col(self.iA)]
            remote(mine, mine, self.gas.at[to], self.gar.at[self.iA], p.peer(self.A, to)).wait_send()
        for off in range(1, self.nB):
            to = lax.rem(self.iB + off, self.nB)
            remote(self.s1.at[to], self.rb.at[self.iB], self.bs.at[to], self.br.at[self.iB], p.peer(self.B, to)).wait_send()
            mine = self.out.at[self.row(self.iB)]
            remote(mine, mine, self.gbs.at[to], self.gbr.at[self.iB], p.peer(self.B, to)).wait_send()
        for off in range(1, self.nC):
            to = lax.rem(self.iC + off, self.nC)
            remote(self.rc.at[self.iC], self.rc.at[self.iC], self.cs.at[to], self.cr.at[self.iC], p.peer(self.C, to)).wait_send()


def reduce_scratch(sizes, order, width):
    nA, nB, nC = (sizes[k] for k in order)
    q = 12 * width // (CORES * nA * nB)
    half = nA * nB
    dma = pltpu.SemaphoreType.DMA
    return [
        pltpu.VMEM((CORES * half, q, width), F32),
        pltpu.VMEM((half, q, width), F32),
        pltpu.VMEM((half, q, width), F32),
        pltpu.VMEM((nA, nB, q, width), F32),
        pltpu.VMEM((nB, q, width), F32),
        pltpu.VMEM((nB, q, width), F32),
        pltpu.VMEM((nC, q, width), F32),
        pltpu.VMEM((CORES * half, q, width), F32),
        dma((2,)), dma((2,)), dma((nA,)), dma((nA,)), dma((nB,)), dma((nB,)), dma((nC,)), dma((nC,)),
        dma((nB,)), dma((nB,)), dma((nA,)), dma((nA,)),
    ]


class Block:
    def __init__(self, place, cols, refs):
        self.p = place
        self.cols = cols
        (self.src, self.pre, self.sw, self.tw, self.gcat, self.pad, self.act, self.slope,
         self.wc, self.wt, self.sh_s, self.sh_r, self.ha_s, self.ha_r) = refs
        self.px, self.w = self.src.shape
        self.step = min(256, self.px)
        self.chunks = self.px // self.step

    def each(self, fn):
        lax.fori_loop(0, self.chunks, lambda i, _: fn(pl.multiple_of(i * self.step, self.step)), None)

    def clear_edges(self):
        p, w = self.p, self.w

        @pl.when(p.v == p.V - 1)
        def _():
            self.gcat[:, : 2 * w] = jnp.zeros((self.px, 2 * w), BF16)

        @pl.when(p.v == p.V - 2)
        def _():
            self.gcat[:, :w] = jnp.zeros((self.px, w), BF16)

        @pl.when(p.s == 0)
        def _():
            self.pad[: self.cols, :] = jnp.zeros((self.cols, 3 * w), BF16)

        @pl.when(p.s == p.S - 1)
        def _():
            self.pad[self.px + self.cols :, :] = jnp.zeros((self.cols, 3 * w), BF16)

    def turn_weights(self):
        w = self.w
        for k in range(3):
            self.wt[k * w : (k + 1) * w, :] = self.tw[k].T
        for ky in range(3):
            for kx in range(3):
                at = (ky * 3 + kx) * w
                self.wc[at : at + w, :] = self.sw[ky, kx].T

    def activate(self):
        def fn(at):
            rows = pl.ds(at, self.step)
            h = self.pre[rows, :].astype(F32)
            sig = jax.nn.sigmoid(h)
            self.act[rows, :] = (h * sig).astype(BF16)
            self.slope[rows, :] = sig * (1.0 + h * (1.0 - sig))

        self.each(fn)

    def shift_copy(self, d, own):
        w = self.w
        dst = self.gcat.at[:, (2 - d) * w : (3 - d) * w]
        return remote(own, dst, self.sh_s.at[d - 1], self.sh_r.at[d - 1], {"video": self.p.v - d})

    def shift_send(self, own):
        for d in (1, 2):

            @pl.when(self.p.v >= d)
            def _():
                self.shift_copy(d, own).start()

    def shift_wait(self):
        w = self.w
        for d in (1, 2):
            there = self.gcat.at[:, (2 - d) * w : (3 - d) * w]

            @pl.when(self.p.v < self.p.V - d)
            def _():
                remote(there, there, self.sh_s.at[d - 1], self.sh_r.at[d - 1], {"video": self.p.v + d}).wait_recv()

    def shift_drain(self, own):
        for d in (1, 2):

            @pl.when(self.p.v >= d)
            def _():
                self.shift_copy(d, own).wait_send()

    def pre_grad(self):
        w, step = self.w, self.step
        col = lax.rem(lax.broadcasted_iota(jnp.int32, (step, w), 0), self.cols)
        first, last = col == 0, col == self.cols - 1

        def fn(at):
            rows = pl.ds(at, step)
            gact = jnp.dot(self.gcat[rows, :], self.wt[...], preferred_element_type=F32)
            gpre = gact.astype(BF16).astype(F32) * self.slope[rows, :]
            to = pl.ds(pl.multiple_of(at + self.cols, self.cols), step)
            self.pad[to, :w] = jnp.where(last, 0.0, pltpu.roll(gpre, step - 1, 0)).astype(BF16)
            self.pad[to, w : 2 * w] = gpre.astype(BF16)
            self.pad[to, 2 * w :] = jnp.where(first, 0.0, pltpu.roll(gpre, 1, 0)).astype(BF16)

        self.each(fn)

    def halo_up(self):
        return remote(self.pad.at[self.cols : 2 * self.cols, :], self.pad.at[self.px + self.cols : self.px + 2 * self.cols, :],
                      self.ha_s.at[0], self.ha_r.at[0], {"section": self.p.s - 1})

    def halo_down(self):
        return remote(self.pad.at[self.px : self.px + self.cols, :], self.pad.at[: self.cols, :],
                      self.ha_s.at[1], self.ha_r.at[1], {"section": self.p.s + 1})

    def halo(self, what):
        p = self.p

        @pl.when(p.s > 0)
        def _():
            if what == "start":
                self.halo_up().start()
            elif what == "recv":
                self.halo_down().wait_recv()
            else:
                self.halo_up().wait_send()

        @pl.when(p.s < p.S - 1)
        def _():
            if what == "start":
                self.halo_down().start()
            elif what == "recv":
                self.halo_up().wait_recv()
            else:
                self.halo_down().wait_send()

    def grad_in(self, out, lanes):
        w, step = self.w, self.step

        def fn(at):
            rows = pl.ds(at, step)
            total = self.gcat[rows, 2 * w :].astype(F32)
            for ky in range(3):
                x = self.pad[pl.ds(pl.multiple_of(at + (2 - ky) * self.cols, self.cols), step), :]
                total = total + jnp.dot(x, self.wc[ky * 3 * w : (ky + 1) * 3 * w, :], preferred_element_type=F32)
            out[rows, lanes] = total.astype(BF16)

        self.each(fn)

    def put(self, part, k, grad):
        w = self.w
        q = part.shape[1]
        rows = jnp.concatenate([grad[:, i * w : (i + 1) * w] for i in range(3)], axis=0)
        n = 3 * w // q
        part[k * n : (k + 1) * n] = rows.reshape(n, q, w)

    def temporal_grad(self, part):
        grad = lax.dot_general(self.act[...], self.gcat[...], (((0,), (0,)), ((), ())), preferred_element_type=F32)
        self.put(part, 3, grad)

    def spatial_grad(self, part):
        left = self.src[...]
        for ky in range(3):
            x = self.pad[(2 - ky) * self.cols : (2 - ky) * self.cols + self.px, :]
            grad = lax.dot_general(left, x, (((0,), (0,)), ((), ())), preferred_element_type=F32)
            self.put(part, ky, grad)


def kernel(sizes, cols, scale, *refs):
    hbm, refs = refs[:9], refs[9:]
    g, in1, pre1, in2, pre2, s1, t1, s2, t2 = hbm
    (gin_out, gs1_out, gt1_out, gs2_out, gt2_out), refs = refs[:5], refs[5:]
    two_refs, refs = refs[:14], refs[14:]
    one_refs, refs = refs[:14], refs[14:]
    r2_refs, refs = refs[:20], refs[20:]
    r1_refs, refs = refs[:20], refs[20:]
    gin, ld, st = refs

    p = Place(sizes)
    two, one = Block(p, cols, two_refs), Block(p, cols, one_refs)
    red2 = Reduce(p, ("z", "x", "y"), scale, r2_refs)
    red1 = Reduce(p, ("x", "y", "z"), scale, r1_refs)
    w = two.w

    barrier = pltpu.get_barrier_semaphore()
    partners = [p.mate()]
    for axis in ("x", "y", "z"):
        partners += [p.peer(axis, lax.rem(p.at[axis] + off, p.n[axis])) for off in range(1, p.n[axis])]
    partners += [{"video": lax.rem(p.v + off, p.V)} for off in (1, 2, p.V - 2, p.V - 1)]
    for to in partners:
        pl.semaphore_signal(barrier, inc=1, device_id=to, device_id_type=MESH)

    own2 = two.gcat.at[:, 2 * w :]
    own1 = one.gcat.at[:, 2 * w :]
    loads = [(pre2, two.pre), (t2, two.tw), (g, own2), (s2, two.sw), (in2, two.src),
             (pre1, one.pre), (t1, one.tw), (s1, one.sw), (in1, one.src)]
    loads = [pltpu.make_async_copy(a, b, ld.at[i]) for i, (a, b) in enumerate(loads)]
    for c in loads:
        c.start()
    two.clear_edges()
    one.clear_edges()
    pl.semaphore_wait(barrier, len(partners))

    two.shift_send(g)
    for c in loads:
        c.wait()
    two.activate()
    two.turn_weights()
    one.activate()
    one.turn_weights()
    two.shift_wait()
    two.pre_grad()
    two.halo("start")
    two.temporal_grad(red2.part)
    two.halo("recv")
    two.grad_in(one.gcat, slice(2 * w, 3 * w))
    one.shift_send(own1)
    two.spatial_grad(red2.part)
    red2.core_send()
    red2.a_send()
    one.shift_wait()
    one.pre_grad()
    one.halo("start")
    one.temporal_grad(red1.part)
    one.halo("recv")
    one.spatial_grad(red1.part)
    red1.core_send()
    one.grad_in(gin, slice(0, w))
    save = pltpu.make_async_copy(gin, gin_out, st.at[0])
    save.start()
    red2.b_send()
    red1.a_send()
    red2.c_send()
    red1.b_send()
    red2.gb_send()
    red1.c_send()
    red2.ga_send()
    red1.gb_send()
    red2.core_gather()
    red1.ga_send()
    red2.finish()
    saves = [save]

    def store(red, s_out, t_out, at):
        n = s_out.shape[0]
        for i, (src, dst) in enumerate(((red.out.at[:n], s_out), (red.out.at[n:], t_out))):
            c = pltpu.make_async_copy(src, dst, st.at[at + i])
            c.start()
            saves.append(c)

    store(red2, gs2_out, gt2_out, 1)
    red1.core_gather()
    red1.finish()
    store(red1, gs1_out, gt1_out, 3)
    two.shift_drain(g)
    one.shift_drain(own1)
    two.halo("drain")
    one.halo("drain")
    red2.drain()
    red1.drain()
    for c in saves:
        c.wait()


def block_scratch(px, cols, w):
    dma = pltpu.SemaphoreType.DMA((2,))
    return [
        pltpu.VMEM((px, w), BF16),
        pltpu.VMEM((px, w), BF16),
        pltpu.VMEM((3, 3, w, w), BF16),
        pltpu.VMEM((3, w, w), BF16),
        pltpu.VMEM((px, 3 * w), BF16),
        pltpu.VMEM((px + 2 * cols, 3 * w), BF16),
        pltpu.VMEM((px, w), BF16),
        pltpu.VMEM((px, w), F32),
        pltpu.VMEM((9 * w, w), BF16),
        pltpu.VMEM((3 * w, w), BF16),
        dma, dma, dma, dma,
    ]


def on_device(sizes, grad_latent, input_one, preact_one, input_two, preact_two,
              spatial_one, temporal_one, spatial_two, temporal_two):
    shape = grad_latent.shape
    rows, cols, w = shape[2:]
    px = rows * cols
    S, V, D = sizes
    scale = 1.0 / math.sqrt(D * V * S * px)
    X = min(XS, V)
    n = {"x": X, "y": V // X * S, "z": D // CORES}
    q2 = 12 * w // (CORES * n["z"] * n["x"])
    q1 = 12 * w // (CORES * n["x"] * n["y"])
    flat = lambda a: a.reshape(px, w)
    hbm = pl.BlockSpec(memory_space=pl.ANY)
    gin, gs1, gt1, gs2, gt2 = pl.pallas_call(
        functools.partial(kernel, sizes, cols, scale),
        out_shape=(
            jax.ShapeDtypeStruct((px, w), BF16),
            jax.ShapeDtypeStruct((9 * w // q1, q1, w), F32),
            jax.ShapeDtypeStruct((3 * w // q1, q1, w), F32),
            jax.ShapeDtypeStruct((9 * w // q2, q2, w), F32),
            jax.ShapeDtypeStruct((3 * w // q2, q2, w), F32),
        ),
        in_specs=[hbm] * 9,
        out_specs=[hbm] * 5,
        scratch_shapes=block_scratch(px, cols, w) + block_scratch(px, cols, w)
        + reduce_scratch(n, ("z", "x", "y"), w) + reduce_scratch(n, ("x", "y", "z"), w)
        + [pltpu.VMEM((px, w), BF16), pltpu.SemaphoreType.DMA((9,)), pltpu.SemaphoreType.DMA((5,))],
        compiler_params=pltpu.CompilerParams(
            collective_id=0, has_side_effects=True, vmem_limit_bytes=60 * 1024 * 1024
        ),
    )(flat(grad_latent), flat(input_one), flat(preact_one), flat(input_two), flat(preact_two),
      spatial_one, temporal_one, spatial_two, temporal_two)
    ss, ts = spatial_one.shape, temporal_one.shape
    return gin.reshape(shape), gs1.reshape(ss), gt1.reshape(ts), gs2.reshape(ss), gt2.reshape(ts)


def solution(mesh):
    sizes = tuple(mesh.shape[k] for k in ("section", "video", "dp"))
    spec = P("dp", "video", "section", None, None)
    return jax.shard_map(
        functools.partial(on_device, sizes),
        mesh=mesh,
        in_specs=(spec,) * 5 + (P(),) * 4,
        out_specs=(spec, P(), P(), P(), P()),
        check_vma=False,
    )
```

```python
import functools
import math

import jax
import jax.numpy as jnp
from jax import lax
from jax.experimental import pallas as pl
from jax.experimental.pallas import tpu as pltpu
from jax.sharding import PartitionSpec as P

MESH = pl.DeviceIdType.MESH
F32 = jnp.float32
BF16 = jnp.bfloat16
XS = 4
CORES = 2
LIMIT = 24 * 1024 * 1024
WIRE = BF16
PARTS = 8
DETOUR = (1, 4, 6)


class Place:
    def __init__(self, sizes):
        self.S, self.V, self.D = sizes
        self.X = min(XS, self.V)
        self.YH = self.V // self.X
        self.Z = self.D // CORES
        self.n = {"x": self.X, "y": self.YH * self.S, "z": self.Z}
        self.s = lax.axis_index("section")
        self.v = lax.axis_index("video")
        self.d = lax.axis_index("dp")
        self.x = lax.rem(self.v, self.X)
        self.yh = lax.div(self.v, self.X)
        self.z = lax.div(self.d, CORES)
        self.c = lax.rem(self.d, CORES)
        self.at = {"x": self.x, "y": self.yh * self.S + self.s, "z": self.z}

    def peer(self, axis, i):
        if axis == "x":
            return {"video": self.yh * self.X + i}
        if axis == "y":
            return {"section": lax.rem(i, self.S), "video": lax.div(i, self.S) * self.X + self.x}
        return {"dp": i * CORES + self.c}

    def mate(self):
        return {"dp": self.z * CORES + (1 - self.c)}


def remote(src, dst, send, recv, to):
    return pltpu.make_async_remote_copy(
        src_ref=src, dst_ref=dst, send_sem=send, recv_sem=recv, device_id=to, device_id_type=MESH
    )


def near(n):
    return sorted(range(1, n), key=lambda o: (min(o, n - o), o))


def far(n):
    return near(n)[::-1]


class Reduce:
    def __init__(self, place, order, scale, refs):
        self.p = place
        self.A, self.B, self.C = order
        self.nA, self.nB, self.nC = (place.n[k] for k in order)
        self.iA, self.iB, self.iC = (place.at[k] for k in order)
        self.scale = scale
        (self.part, self.rcore, self.own, self.s0, self.ra, self.s1, self.rb, self.rc, self.out,
         self.ms, self.mr, self.as_, self.ar, self.bs, self.br, self.cs, self.cr,
         self.gbs, self.gbr, self.gas, self.gar, self.gms, self.gmr) = refs
        self.half = self.nA * self.nB

    def a(self, off):
        return lax.rem(self.iA + off, self.nA)

    def b(self, off):
        return lax.rem(self.iB + off, self.nB)

    def c(self, off):
        return lax.rem(self.iC + off, self.nC)

    def core_copy(self, a):
        rows = pl.ds(a * self.nB, self.nB)
        return remote(self.part.at[pl.ds((1 - self.p.c) * self.half + a * self.nB, self.nB)], self.rcore.at[rows],
                      self.ms.at[a], self.mr.at[a], self.p.mate())

    def core_send(self):
        for off in far(self.nA) + [0]:
            self.core_copy(self.a(off)).start()

    def a_copy(self, to, b):
        return remote(self.s0.at[to, b], self.ra.at[self.iA, b], self.as_.at[to, b], self.ar.at[self.iA, b],
                      self.p.peer(self.A, to))

    def a_send(self):
        for off in far(self.nA) + [0]:
            a = self.a(off)
            self.core_copy(a).wait_recv()
            total = self.part[pl.ds(self.p.c * self.half + a * self.nB, self.nB)] + self.rcore[pl.ds(a * self.nB, self.nB)]
            if off == 0:
                self.own[...] = total
            else:
                self.s0[a] = total.astype(self.s0.dtype)
                for ob in far(self.nB) + [0]:
                    self.a_copy(a, self.b(ob)).start()

    def b_copy(self, to):
        return remote(self.s1.at[to], self.rb.at[self.iB], self.bs.at[to], self.br.at[self.iB], self.p.peer(self.B, to))

    def b_send(self):
        for ob in far(self.nB) + [0]:
            b = self.b(ob)
            total = self.own[b]
            for off in near(self.nA):
                frm = self.a(off)
                there = self.ra.at[frm, b]
                remote(there, there, self.as_.at[frm, b], self.ar.at[frm, b], self.p.peer(self.A, frm)).wait_recv()
                total = total + there[...].astype(F32)
            if ob == 0:
                self.own[b] = total
            else:
                self.s1[b] = total.astype(self.s1.dtype)
                self.b_copy(b).start()

    def c_copy(self, to):
        mine = self.rc.at[self.iC]
        return remote(mine, mine, self.cs.at[to], self.cr.at[self.iC], self.p.peer(self.C, to))

    def c_send(self):
        total = self.own[self.iB]
        for ob in near(self.nB):
            frm = self.b(ob)
            there = self.rb.at[frm]
            remote(there, there, self.bs.at[frm], self.br.at[frm], self.p.peer(self.B, frm)).wait_recv()
            total = total + there[...].astype(F32)
        self.rc[self.iC] = total.astype(self.rc.dtype)
        for off in far(self.nC):
            self.c_copy(self.c(off)).start()

    def gb_copy(self, to):
        mine = self.out.at[self.p.c * self.nA + self.iA, self.iB]
        return remote(mine, mine, self.gbs.at[to], self.gbr.at[self.iB], self.p.peer(self.B, to))

    def gb_send(self):
        for off in near(self.nC):
            frm = self.c(off)
            there = self.rc.at[frm]
            remote(there, there, self.cs.at[frm], self.cr.at[frm], self.p.peer(self.C, frm)).wait_recv()
        total = self.rc[0].astype(F32)
        for i in range(1, self.nC):
            total = total + self.rc[i].astype(F32)
        self.out[self.p.c * self.nA + self.iA, self.iB] = (total * self.scale).astype(self.out.dtype)
        for ob in far(self.nB):
            self.gb_copy(self.b(ob)).start()

    def ga_copy(self, to, b):
        mine = self.out.at[self.p.c * self.nA + self.iA, b]
        return remote(mine, mine, self.gas.at[to, b], self.gar.at[self.iA, b], self.p.peer(self.A, to))

    def ga_send(self):
        for ob in [0] + near(self.nB):
            b = self.b(ob)
            if ob:
                there = self.out.at[self.p.c * self.nA + self.iA, b]
                remote(there, there, self.gbs.at[b], self.gbr.at[b], self.p.peer(self.B, b)).wait_recv()
            for off in far(self.nA):
                self.ga_copy(self.a(off), b).start()

    def gm_copy(self, b):
        mine = self.out.at[pl.ds(self.p.c * self.nA, self.nA), b]
        return remote(mine, mine, self.gms.at[b], self.gmr.at[b], self.p.mate())

    def core_gather(self):
        for ob in [0] + near(self.nB):
            b = self.b(ob)
            for off in near(self.nA):
                frm = self.a(off)
                there = self.out.at[self.p.c * self.nA + frm, b]
                remote(there, there, self.gas.at[frm, b], self.gar.at[frm, b], self.p.peer(self.A, frm)).wait_recv()
            self.gm_copy(b).start()

    def finish(self):
        for ob in [0] + near(self.nB):
            b = self.b(ob)
            there = self.out.at[pl.ds((1 - self.p.c) * self.nA, self.nA), b]
            remote(there, there, self.gms.at[b], self.gmr.at[b], self.p.mate()).wait_recv()

    def drain(self):
        for a in range(self.nA):
            self.core_copy(a).wait_send()
        for off in near(self.nA):
            a = self.a(off)
            for b in range(self.nB):
                self.a_copy(a, b).wait_send()
                self.ga_copy(a, b).wait_send()
        for ob in near(self.nB):
            b = self.b(ob)
            self.b_copy(b).wait_send()
            self.gb_copy(b).wait_send()
        for off in near(self.nC):
            self.c_copy(self.c(off)).wait_send()
        for b in range(self.nB):
            self.gm_copy(b).wait_send()


def reduce_scratch(sizes, order, width):
    nA, nB, nC = (sizes[k] for k in order)
    q = 12 * width // (CORES * nA * nB)
    half = nA * nB
    dma = pltpu.SemaphoreType.DMA
    return [
        pltpu.VMEM((CORES * half, q, width), F32),
        pltpu.VMEM((half, q, width), F32),
        pltpu.VMEM((nB, q, width), F32),
        pltpu.VMEM((nA, nB, q, width), WIRE),
        pltpu.VMEM((nA, nB, q, width), WIRE),
        pltpu.VMEM((nB, q, width), WIRE),
        pltpu.VMEM((nB, q, width), WIRE),
        pltpu.VMEM((nC, q, width), WIRE),
    ], [
        dma((nA,)), dma((nA,)), dma((nA, nB)), dma((nA, nB)), dma((nB,)), dma((nB,)), dma((nC,)), dma((nC,)),
        dma((nB,)), dma((nB,)), dma((nA, nB)), dma((nA, nB)), dma((nB,)), dma((nB,)),
    ]


class Block:
    def __init__(self, place, cols, order, refs):
        self.p = place
        self.cols = cols
        (self.src, self.pre, self.sw, self.tw, self.gcat, self.pad, self.act, self.slope,
         self.wc, self.wt, self.hop, self.sh_s, self.sh_r, self.ha_s, self.ha_r) = refs
        self.px, self.w = self.src.shape
        self.chunks = 4
        self.step = self.px // self.chunks
        self.msg = self.px // PARTS
        self.order = order
        per = PARTS // self.chunks
        self.sends = [c * per + i for c in order for i in range(per)]

    def each(self, fn, order=None):
        for i in range(self.chunks) if order is None else order:
            fn(i * self.step)

    def clear_edges(self):
        p, w = self.p, self.w

        @pl.when(p.v == p.V - 1)
        def _():
            self.gcat[:, : 2 * w] = jnp.zeros((self.px, 2 * w), BF16)

        @pl.when(p.v == p.V - 2)
        def _():
            self.gcat[:, :w] = jnp.zeros((self.px, w), BF16)

        @pl.when(p.s == 0)
        def _():
            self.pad[: self.cols, :] = jnp.zeros((self.cols, 3 * w), BF16)

        @pl.when(p.s == p.S - 1)
        def _():
            self.pad[self.px + self.cols :, :] = jnp.zeros((self.cols, 3 * w), BF16)

    def turn_weights(self):
        w = self.w
        for k in range(3):
            self.wt[k * w : (k + 1) * w, :] = self.tw[k].T
        for ky in range(3):
            for kx in range(3):
                at = (ky * 3 + kx) * w
                self.wc[at : at + w, :] = self.sw[ky, kx].T

    def activate(self):
        def fn(at):
            rows = pl.ds(at, self.step)
            h = self.pre[rows, :].astype(F32)
            sig = jax.nn.sigmoid(h)
            self.act[rows, :] = (h * sig).astype(BF16)
            self.slope[rows, :] = sig * (1.0 + h * (1.0 - sig))

        self.each(fn)


    def rows(self, m):
        return pl.ds(m * self.msg, self.msg)

    def slot(self, d, m):
        return self.gcat.at[self.rows(m), (2 - d) * self.w : (3 - d) * self.w]

    def to_slot(self, kind, src, d, m, back):
        return remote(src, self.slot(d, m), self.sh_s.at[kind, m], self.sh_r.at[d, m], {"video": self.p.v - back})

    def direct(self, own, d, m):
        return self.to_slot(d, own.at[self.rows(m)], d, m, d)

    def aside(self, own, d, m, ahead):
        hop = self.hop.at[self.rows(m)]
        return remote(own.at[self.rows(m)], hop, self.sh_s.at[d, m], self.sh_r.at[0, m], {"video": self.p.v + ahead})

    def relay_copy(self, d, m, back):
        return self.to_slot(0, self.hop.at[self.rows(m)], d, m, back)

    def forward_copy(self, m):
        return self.to_slot(0, self.slot(1, m), 2, m, 1)

    def shift_do(self, own, what, sends=None):
        p = self.p
        sends = self.sends if sends is None else sends
        last = p.X - 1

        def act(copy):
            if what == "start":
                copy.start()
            else:
                copy.wait_send()

        for d in (1, 2):

            @pl.when(p.x >= d)
            def _():
                for m in sends:
                    act(self.direct(own, d, m))

            @pl.when((p.yh >= 1) & (p.x == d - 1))
            def _():
                for m in sends:
                    if m in self.detour:
                        act(self.aside(own, d, m, last if d == 1 else 1))
                    else:
                        act(self.direct(own, d, m))

    @property
    def detour(self):
        return [self.sends[i] for i in DETOUR]

    def shift_send(self, own, sends=None):
        self.shift_do(own, "start", sends)

    def shift_drain(self, own):
        p = self.p
        last = p.X - 1
        self.shift_do(own, "wait")
        for d in (1, 2):

            @pl.when((p.yh >= 1) & (p.x == p.X - d))
            def _():
                for m in self.detour:
                    self.relay_copy(d, m, p.X if d == 1 else p.X - 1).wait_send()

        @pl.when((p.yh < p.YH - 1) & (p.x == last))
        def _():
            for m in self.sends:
                self.forward_copy(m).wait_send()

    def relay(self):
        p = self.p
        for d in (1, 2):

            @pl.when((p.yh >= 1) & (p.x == p.X - d))
            def _():
                for m in self.detour:
                    there = self.hop.at[self.rows(m)]
                    remote(there, there, self.sh_s.at[0, m], self.sh_r.at[0, m], {"video": p.v - 1}).wait_recv()
                    self.relay_copy(d, m, p.X if d == 1 else p.X - 1).start()

    def got(self, d, m):
        there = self.slot(d, m)
        remote(there, there, self.sh_s.at[d, m], self.sh_r.at[d, m], {"video": self.p.v - 1}).wait_recv()

    def forward(self):
        p = self.p

        @pl.when((p.yh < p.YH - 1) & (p.x == p.X - 1))
        def _():
            for m in self.sends:
                self.got(1, m)
                self.forward_copy(m).start()

    def shift_wait(self, sends):
        p = self.p

        @pl.when(p.x < p.X - 1)
        def _():
            for m in sends:
                self.got(1, m)

        @pl.when(p.v < p.V - 2)
        def _():
            for m in sends:
                self.got(2, m)

    def messages(self, chunk):
        per = PARTS // self.chunks
        return [chunk * per + i for i in range(per)]

    def pre_grad(self, chunks):
        w, step = self.w, self.step
        col = lax.rem(lax.broadcasted_iota(jnp.int32, (step, w), 0), self.cols)
        first, last = col == 0, col == self.cols - 1

        def fn(at):
            rows = pl.ds(at, step)
            gact = jnp.dot(self.gcat[rows, :], self.wt[...], preferred_element_type=F32)
            gpre = gact.astype(BF16).astype(F32) * self.slope[rows, :]
            to = pl.ds(at + self.cols, step)
            self.pad[to, :w] = jnp.where(last, 0.0, pltpu.roll(gpre, step - 1, 0)).astype(BF16)
            self.pad[to, w : 2 * w] = gpre.astype(BF16)
            self.pad[to, 2 * w :] = jnp.where(first, 0.0, pltpu.roll(gpre, 1, 0)).astype(BF16)

        for i in chunks:
            self.shift_wait(self.messages(i))
            fn(i * step)

    def halo_up(self):
        return remote(self.pad.at[self.cols : 2 * self.cols, :], self.pad.at[self.px + self.cols : self.px + 2 * self.cols, :],
                      self.ha_s.at[0], self.ha_r.at[0], {"section": self.p.s - 1})

    def halo_down(self):
        return remote(self.pad.at[self.px : self.px + self.cols, :], self.pad.at[: self.cols, :],
                      self.ha_s.at[1], self.ha_r.at[1], {"section": self.p.s + 1})

    def halo(self, what):
        p = self.p

        @pl.when(p.s > 0)
        def _():
            if what == "start":
                self.halo_up().start()
            elif what == "recv":
                self.halo_down().wait_recv()
            else:
                self.halo_up().wait_send()

        @pl.when(p.s < p.S - 1)
        def _():
            if what == "start":
                self.halo_down().start()
            elif what == "recv":
                self.halo_up().wait_recv()
            else:
                self.halo_down().wait_send()

    def grad_in(self, out, lanes, chunks):
        w, step = self.w, self.step

        def fn(at):
            rows = pl.ds(at, step)
            total = self.gcat[rows, 2 * w :].astype(F32)
            for ky in range(3):
                x = self.pad[pl.ds(at + (2 - ky) * self.cols, step), :]
                total = total + jnp.dot(x, self.wc[ky * 3 * w : (ky + 1) * 3 * w, :], preferred_element_type=F32)
            out[rows, lanes] = total.astype(BF16)

        self.each(fn, chunks)

    def put(self, part, k, grad):
        w = self.w
        q = part.shape[1]
        rows = jnp.concatenate([grad[:, i * w : (i + 1) * w] for i in range(3)], axis=0)
        n = 3 * w // q
        part[k * n : (k + 1) * n] = rows.reshape(n, q, w)

    def temporal_grad(self, part):
        grad = lax.dot_general(self.act[...], self.gcat[...], (((0,), (0,)), ((), ())), preferred_element_type=F32)
        self.put(part, 3, grad)

    def spatial_grad(self, part):
        left = self.src[...]
        for ky in range(3):
            x = self.pad[(2 - ky) * self.cols : (2 - ky) * self.cols + self.px, :]
            grad = lax.dot_general(left, x, (((0,), (0,)), ((), ())), preferred_element_type=F32)
            self.put(part, ky, grad)


def kernel(sizes, cols, scale, *refs):
    g, in1, pre1, in2, pre2, s1, t1, s2, t2 = refs[:9]
    gin, out1, out2 = refs[9:12]
    refs = refs[12:]
    two_refs, refs = refs[:15], refs[15:]
    one_refs, refs = refs[:15], refs[15:]
    r2_refs, refs = refs[:8] + (out2,) + refs[8:22], refs[22:]
    r1_refs, refs = refs[:8] + (out1,) + refs[8:22], refs[22:]
    (ld,) = refs

    p = Place(sizes)
    two, one = Block(p, cols, (0, 3, 1, 2), two_refs), Block(p, cols, (1, 2, 0, 3), one_refs)
    red2 = Reduce(p, ("z", "x", "y"), scale, r2_refs)
    red1 = Reduce(p, ("x", "y", "z"), scale, r1_refs)
    w = two.w

    barrier = pltpu.get_barrier_semaphore()
    partners = [p.mate()]
    for axis in ("x", "y", "z"):
        partners += [p.peer(axis, lax.rem(p.at[axis] + off, p.n[axis])) for off in far(p.n[axis])]
    partners += [{"video": lax.rem(p.v + off, p.V)} for off in (1, 2, 3, p.V - 3, p.V - 2, p.V - 1)]
    for to in partners:
        pl.semaphore_signal(barrier, inc=1, device_id=to, device_id_type=MESH)

    own2 = two.gcat.at[:, 2 * w :]
    own1 = one.gcat.at[:, 2 * w :]
    loads = [(pre2, two.pre), (t2, two.tw), (g, own2), (s2, two.sw), (in2, two.src),
             (pre1, one.pre), (t1, one.tw), (s1, one.sw), (in1, one.src)]
    loads = [pltpu.make_async_copy(a, b, ld.at[i]) for i, (a, b) in enumerate(loads)]
    for c in loads:
        c.start()
    two.clear_edges()
    one.clear_edges()
    pl.semaphore_wait(barrier, len(partners))

    two.shift_send(g)
    for c in loads:
        c.wait()
    two.activate()
    two.relay()
    two.turn_weights()
    one.activate()
    one.turn_weights()
    two.forward()
    two.pre_grad((0, 3))
    two.halo("start")
    two.pre_grad((1, 2))
    two.temporal_grad(red2.part)
    for chunk in (1, 2):
        two.grad_in(one.gcat, slice(2 * w, 3 * w), (chunk,))
        one.shift_send(own1, one.messages(chunk))
    two.halo("recv")
    for chunk in (0, 3):
        two.grad_in(one.gcat, slice(2 * w, 3 * w), (chunk,))
        one.shift_send(own1, one.messages(chunk))
    one.relay()
    two.spatial_grad(red2.part)
    red2.core_send()
    one.forward()
    red2.a_send()
    one.pre_grad((1, 2, 0, 3))
    one.halo("start")
    one.temporal_grad(red1.part)
    one.halo("recv")
    one.spatial_grad(red1.part)
    red1.core_send()
    one.grad_in(gin, slice(0, w), (0, 1, 2, 3))
    red2.b_send()
    red1.a_send()
    red2.c_send()
    red1.b_send()
    red2.gb_send()
    red1.c_send()
    red2.ga_send()
    red1.gb_send()
    red2.core_gather()
    red1.ga_send()
    red2.finish()
    red1.core_gather()
    red1.finish()
    two.shift_drain(g)
    one.shift_drain(own1)
    two.halo("drain")
    one.halo("drain")
    red2.drain()
    red1.drain()


def store_kernel(gin, out1, out2, gin_to, gs1_to, gt1_to, gs2_to, gt2_to, wide1, wide2, sem):
    copies = [pltpu.make_async_copy(gin, gin_to, sem.at[0])]
    copies[0].start()
    for k, (src, wide, s_to, t_to) in enumerate(((out1, wide1, gs1_to, gt1_to), (out2, wide2, gs2_to, gt2_to))):
        wide[...] = src[...].astype(F32)
        n = s_to.shape[0]
        for i, (a, b) in enumerate(((wide.at[:n], s_to), (wide.at[n:], t_to))):
            c = pltpu.make_async_copy(a, b, sem.at[1 + 2 * k + i])
            c.start()
            copies.append(c)
    for c in copies:
        c.wait()


def block_scratch(px, cols, w):
    dma = pltpu.SemaphoreType.DMA((2,))
    many = pltpu.SemaphoreType.DMA((3, PARTS))
    return [
        pltpu.VMEM((px, w), BF16),
        pltpu.VMEM((px, w), BF16),
        pltpu.VMEM((3, 3, w, w), BF16),
        pltpu.VMEM((3, w, w), BF16),
        pltpu.VMEM((px, 3 * w), BF16),
        pltpu.VMEM((px + 2 * cols, 3 * w), BF16),
        pltpu.VMEM((px, w), BF16),
        pltpu.VMEM((px, w), F32),
        pltpu.VMEM((9 * w, w), BF16),
        pltpu.VMEM((3 * w, w), BF16),
        pltpu.VMEM((px, w), BF16),
        many, many, dma, dma,
    ]


def on_device(sizes, grad_latent, input_one, preact_one, input_two, preact_two,
              spatial_one, temporal_one, spatial_two, temporal_two):
    shape = grad_latent.shape
    rows, cols, w = shape[2:]
    px = rows * cols
    S, V, D = sizes
    scale = 1.0 / math.sqrt(D * V * S * px)
    X = min(XS, V)
    n = {"x": X, "y": V // X * S, "z": D // CORES}
    order1, order2 = ("x", "y", "z"), ("z", "x", "y")
    v1, k1 = reduce_scratch(n, order1, w)
    v2, k2 = reduce_scratch(n, order2, w)
    stay = lambda a: pltpu.with_memory_space_constraint(a, pltpu.HBM)
    flat = lambda a: stay(a.reshape(px, w))
    hbm = pl.BlockSpec(memory_space=pl.ANY)
    vmem = pl.BlockSpec(memory_space=pltpu.VMEM)
    sums = [jax.ShapeDtypeStruct((CORES * v[3].shape[0],) + v[3].shape[1:], WIRE) for v in (v1, v2)]
    gin, out1, out2 = pl.pallas_call(
        functools.partial(kernel, sizes, cols, scale),
        out_shape=(jax.ShapeDtypeStruct((px, w), BF16), *sums),
        in_specs=[pl.BlockSpec(memory_space=pltpu.HBM)] * 9,
        out_specs=[vmem] * 3,
        scratch_shapes=block_scratch(px, cols, w) + block_scratch(px, cols, w)
        + v2 + k2 + v1 + k1 + [pltpu.SemaphoreType.DMA((9,))],
        compiler_params=pltpu.CompilerParams(
            collective_id=0, has_side_effects=True, vmem_limit_bytes=LIMIT
        ),
    )(flat(grad_latent), flat(input_one), flat(preact_one), flat(input_two), flat(preact_two),
      stay(spatial_one), stay(temporal_one), stay(spatial_two), stay(temporal_two))
    tile = lambda a: a.reshape((a.shape[0] * a.shape[1],) + a.shape[2:])
    out1, out2 = tile(out1), tile(out2)
    f32 = lambda a, tiles: jax.ShapeDtypeStruct((tiles * w // a.shape[1],) + a.shape[1:], F32)
    gin, gs1, gt1, gs2, gt2 = pl.pallas_call(
        store_kernel,
        out_shape=(jax.ShapeDtypeStruct((px, w), BF16), f32(out1, 9), f32(out1, 3), f32(out2, 9), f32(out2, 3)),
        in_specs=[vmem] * 3,
        out_specs=[hbm] * 5,
        scratch_shapes=[pltpu.VMEM(out1.shape, F32), pltpu.VMEM(out2.shape, F32), pltpu.SemaphoreType.DMA((5,))],
        compiler_params=pltpu.CompilerParams(vmem_limit_bytes=8 * 1024 * 1024),
    )(gin, out1, out2)
    ss, ts = spatial_one.shape, temporal_one.shape
    return gin.reshape(shape), gs1.reshape(ss), gt1.reshape(ts), gs2.reshape(ss), gt2.reshape(ts)


def solution(mesh):
    sizes = tuple(mesh.shape[k] for k in ("section", "video", "dp"))
    spec = P("dp", "video", "section", None, None)
    return jax.shard_map(
        functools.partial(on_device, sizes),
        mesh=mesh,
        in_specs=(spec,) * 5 + (P(),) * 4,
        out_specs=(spec, P(), P(), P(), P()),
        check_vma=False,
    )
```

```python
import functools
import math

import jax
import jax.numpy as jnp
from jax import lax
from jax.experimental import pallas as pl
from jax.experimental.pallas import tpu as pltpu
from jax.sharding import PartitionSpec as P

MESH = pl.DeviceIdType.MESH
F32 = jnp.float32
BF16 = jnp.bfloat16
XS = 4
CORES = 2
LIMIT = 24 * 1024 * 1024
WIRE = BF16
GROUPS = 1
PARTS = 8
DETOUR_TWO = (3, 4, 5)
DETOUR_ONE = (2, 3, 4)


class Place:
    def __init__(self, sizes):
        self.S, self.V, self.D = sizes
        self.X = min(XS, self.V)
        self.YH = self.V // self.X
        self.Z = self.D // CORES
        self.n = {"x": self.X, "y": self.YH * self.S, "z": self.Z}
        self.s = lax.axis_index("section")
        self.v = lax.axis_index("video")
        self.d = lax.axis_index("dp")
        self.x = lax.rem(self.v, self.X)
        self.yh = lax.div(self.v, self.X)
        self.z = lax.div(self.d, CORES)
        self.c = lax.rem(self.d, CORES)
        self.at = {"x": self.x, "y": self.yh * self.S + self.s, "z": self.z}

    def peer(self, axis, i):
        if axis == "x":
            return {"video": self.yh * self.X + i}
        if axis == "y":
            return {"section": lax.rem(i, self.S), "video": lax.div(i, self.S) * self.X + self.x}
        return {"dp": i * CORES + self.c}

    def mate(self):
        return {"dp": self.z * CORES + (1 - self.c)}


def remote(src, dst, send, recv, to):
    return pltpu.make_async_remote_copy(
        src_ref=src, dst_ref=dst, send_sem=send, recv_sem=recv, device_id=to, device_id_type=MESH
    )


def near(n):
    return sorted(range(1, n), key=lambda o: (min(o, n - o), o))


def far(n):
    return near(n)[::-1]


class Reduce:
    def __init__(self, place, order, scale, refs):
        self.p = place
        self.A, self.B, self.C = order
        self.nA, self.nB, self.nC = (place.n[k] for k in order)
        self.iA, self.iB, self.iC = (place.at[k] for k in order)
        self.scale = scale
        (self.part, self.rcore, self.own, self.s0, self.ra, self.s1, self.rb, self.rc, self.out,
         self.ms, self.mr, self.as_, self.ar, self.bs, self.br, self.cs, self.cr,
         self.gbs, self.gbr, self.gas, self.gar, self.gms, self.gmr) = refs
        self.half = self.nA * self.nB

    def a(self, off):
        return lax.rem(self.iA + off, self.nA)

    def b(self, off):
        return lax.rem(self.iB + off, self.nB)

    def c(self, off):
        return lax.rem(self.iC + off, self.nC)

    def core_copy(self, a):
        rows = pl.ds(a * self.nB, self.nB)
        return remote(self.part.at[pl.ds((1 - self.p.c) * self.half + a * self.nB, self.nB)], self.rcore.at[rows],
                      self.ms.at[a], self.mr.at[a], self.p.mate())

    def core_send(self):
        for off in far(self.nA) + [0]:
            self.core_copy(self.a(off)).start()

    def core_send_part(self, k):
        @pl.when(self.p.c == 1 - k // 2)
        def _():
            for a in range(k % 2 * self.nA // 2, (k % 2 + 1) * self.nA // 2):
                self.core_copy(a).start()

    def some(self, og):
        size = self.nB // GROUPS
        return lax.rem(lax.div(self.iB, size) + og, GROUPS), size

    def a_copy(self, to, g):
        rows = pl.ds(g * (self.nB // GROUPS), self.nB // GROUPS)
        return remote(self.s0.at[to, rows], self.ra.at[self.iA, rows], self.as_.at[to, g], self.ar.at[self.iA, g],
                      self.p.peer(self.A, to))

    def a_send(self):
        for off in far(self.nA) + [0]:
            a = self.a(off)
            self.core_copy(a).wait_recv()
            total = self.part[pl.ds(self.p.c * self.half + a * self.nB, self.nB)] + self.rcore[pl.ds(a * self.nB, self.nB)]
            if off == 0:
                self.own[...] = total
            else:
                self.s0[a] = total.astype(self.s0.dtype)
                for og in reversed(range(GROUPS)):
                    self.a_copy(a, self.some(og)[0]).start()

    def b_copy(self, to):
        return remote(self.s1.at[to], self.rb.at[self.iB], self.bs.at[to], self.br.at[self.iB], self.p.peer(self.B, to))

    def b_send(self):
        for og in reversed(range(GROUPS)):
            g, size = self.some(og)
            rows = pl.ds(g * size, size)
            total = self.own[rows]
            for off in near(self.nA):
                frm = self.a(off)
                there = self.ra.at[frm, rows]
                remote(there, there, self.as_.at[frm, g], self.ar.at[frm, g], self.p.peer(self.A, frm)).wait_recv()
                total = total + there[...].astype(F32)
            self.own[rows] = total
            self.s1[rows] = total.astype(self.s1.dtype)
            for i in range(size):
                if GROUPS == 1:
                    if i:
                        self.b_copy(self.b(far(size)[i - 1])).start()
                else:
                    b = g * size + i

                    @pl.when(b != self.iB)
                    def _():
                        self.b_copy(b).start()

    def b_copy(self, to):
        return remote(self.s1.at[to], self.rb.at[self.iB], self.bs.at[to], self.br.at[self.iB], self.p.peer(self.B, to))

    def c_copy(self, to):
        mine = self.rc.at[self.iC]
        return remote(mine, mine, self.cs.at[to], self.cr.at[self.iC], self.p.peer(self.C, to))

    def c_send(self):
        total = self.own[self.iB]
        for ob in near(self.nB):
            frm = self.b(ob)
            there = self.rb.at[frm]
            remote(there, there, self.bs.at[frm], self.br.at[frm], self.p.peer(self.B, frm)).wait_recv()
            total = total + there[...].astype(F32)
        self.rc[self.iC] = total.astype(self.rc.dtype)
        for off in far(self.nC):
            self.c_copy(self.c(off)).start()

    def gb_copy(self, to):
        mine = self.out.at[self.p.c * self.nA + self.iA, self.iB]
        return remote(mine, mine, self.gbs.at[to], self.gbr.at[self.iB], self.p.peer(self.B, to))

    def gb_send(self):
        for off in near(self.nC):
            frm = self.c(off)
            there = self.rc.at[frm]
            remote(there, there, self.cs.at[frm], self.cr.at[frm], self.p.peer(self.C, frm)).wait_recv()
        total = self.rc[0].astype(F32)
        for i in range(1, self.nC):
            total = total + self.rc[i].astype(F32)
        self.out[self.p.c * self.nA + self.iA, self.iB] = (total * self.scale).astype(self.out.dtype)
        for ob in far(self.nB):
            self.gb_copy(self.b(ob)).start()

    def ga_copy(self, to, g):
        mine = self.out.at[self.p.c * self.nA + self.iA, pl.ds(g * (self.nB // GROUPS), self.nB // GROUPS)]
        return remote(mine, mine, self.gas.at[to, g], self.gar.at[self.iA, g], self.p.peer(self.A, to))

    def gb_wait(self, b):
        there = self.out.at[self.p.c * self.nA + self.iA, b]
        remote(there, there, self.gbs.at[b], self.gbr.at[b], self.p.peer(self.B, b)).wait_recv()

    def ga_send(self):
        for og in range(GROUPS):
            g, size = self.some(og)
            for i in range(size):
                if GROUPS == 1:
                    if i:
                        self.gb_wait(self.b(near(size)[i - 1]))
                else:
                    b = g * size + i

                    @pl.when(b != self.iB)
                    def _():
                        self.gb_wait(b)

            for off in far(self.nA):
                self.ga_copy(self.a(off), g).start()

    def gm_copy(self, g, c):
        mine = self.out.at[pl.ds(c * self.nA, self.nA), pl.ds(g * (self.nB // GROUPS), self.nB // GROUPS)]
        return remote(mine, mine, self.gms.at[g], self.gmr.at[g], self.p.mate())

    def core_gather(self):
        for og in range(GROUPS):
            g, size = self.some(og)
            for off in near(self.nA):
                frm = self.a(off)
                there = self.out.at[self.p.c * self.nA + frm, pl.ds(g * size, size)]
                remote(there, there, self.gas.at[frm, g], self.gar.at[frm, g], self.p.peer(self.A, frm)).wait_recv()
            self.gm_copy(g, self.p.c).start()

    def finish(self):
        for og in range(GROUPS):
            self.gm_copy(self.some(og)[0], 1 - self.p.c).wait_recv()

    def drain(self):
        for a in range(self.nA):
            self.core_copy(a).wait_send()
        for off in near(self.nA):
            a = self.a(off)
            for g in range(GROUPS):
                self.a_copy(a, g).wait_send()
                self.ga_copy(a, g).wait_send()
        for ob in near(self.nB):
            b = self.b(ob)
            self.b_copy(b).wait_send()
            self.gb_copy(b).wait_send()
        for off in near(self.nC):
            self.c_copy(self.c(off)).wait_send()
        for g in range(GROUPS):
            self.gm_copy(g, self.p.c).wait_send()


def reduce_scratch(sizes, order, width):
    nA, nB, nC = (sizes[k] for k in order)
    q = 12 * width // (CORES * nA * nB)
    half = nA * nB
    dma = pltpu.SemaphoreType.DMA
    return [
        pltpu.VMEM((CORES * half, q, width), F32),
        pltpu.VMEM((half, q, width), F32),
        pltpu.VMEM((nB, q, width), F32),
        pltpu.VMEM((nA, nB, q, width), WIRE),
        pltpu.VMEM((nA, nB, q, width), WIRE),
        pltpu.VMEM((nB, q, width), WIRE),
        pltpu.VMEM((nB, q, width), WIRE),
        pltpu.VMEM((nC, q, width), WIRE),
    ], [
        dma((nA,)), dma((nA,)), dma((nA, GROUPS)), dma((nA, GROUPS)), dma((nB,)), dma((nB,)), dma((nC,)), dma((nC,)),
        dma((nB,)), dma((nB,)), dma((nA, GROUPS)), dma((nA, GROUPS)), dma((GROUPS,)), dma((GROUPS,)),
    ]


class Block:
    def __init__(self, place, cols, order, detour, refs):
        self.p = place
        self.cols = cols
        (self.src, self.pre, self.sw, self.tw, self.gcat, self.pad, self.act, self.slope,
         self.wc, self.wt, self.hop, self.src_t, self.act_t, self.early,
         self.sh_s, self.sh_r, self.ha_s, self.ha_r, self.in_s, self.in_r) = refs
        self.px, self.w = self.pre.shape
        self.chunks = 4
        self.step = self.px // self.chunks
        self.msg = self.px // PARTS
        self.order = order
        self.detour = detour
        self.sends = [m for c in order for m in self.messages(c)]

    def each(self, fn, order=None):
        for i in range(self.chunks) if order is None else order:
            fn(i * self.step)

    def clear_edges(self):
        p, w = self.p, self.w

        @pl.when(p.v == p.V - 1)
        def _():
            self.gcat[:, : 2 * w] = jnp.zeros((self.px, 2 * w), BF16)

        @pl.when(p.v == p.V - 2)
        def _():
            self.gcat[:, :w] = jnp.zeros((self.px, w), BF16)

        @pl.when(p.s == 0)
        def _():
            self.pad[: self.cols, :] = jnp.zeros((self.cols, 3 * w), BF16)
            self.src[: self.cols, :] = jnp.zeros((self.cols, w), BF16)

        @pl.when(p.s == p.S - 1)
        def _():
            self.pad[self.px + self.cols :, :] = jnp.zeros((self.cols, 3 * w), BF16)
            self.src[self.px + self.cols :, :] = jnp.zeros((self.cols, w), BF16)

    def turn_weights(self):
        w = self.w
        for k in range(3):
            self.wt[k * w : (k + 1) * w, :] = self.tw[k].T
        for ky in range(3):
            for kx in range(3):
                at = (ky * 3 + kx) * w
                self.wc[at : at + w, :] = self.sw[ky, kx].T

    def activate(self):
        def fn(at):
            rows = pl.ds(at, self.step)
            h = self.pre[rows, :].astype(F32)
            sig = jax.nn.sigmoid(h)
            self.act[rows, :] = (h * sig).astype(BF16)
            self.slope[rows, :] = sig * (1.0 + h * (1.0 - sig))

        self.each(fn)


    def rows(self, m):
        return pl.ds(m * self.msg, self.msg)

    def slot(self, d, m):
        return self.gcat.at[self.rows(m), (2 - d) * self.w : (3 - d) * self.w]

    def to_slot(self, kind, src, d, m, back):
        return remote(src, self.slot(d, m), self.sh_s.at[kind, m], self.sh_r.at[d, m], {"video": self.p.v - back})

    def direct(self, own, d, m):
        return self.to_slot(d, own.at[self.rows(m)], d, m, d)

    def aside(self, own, d, m, ahead):
        hop = self.hop.at[self.rows(m)]
        return remote(own.at[self.rows(m)], hop, self.sh_s.at[d, m], self.sh_r.at[0, m], {"video": self.p.v + ahead})

    def relay_copies(self, d, m):
        hop, X = self.hop.at[self.rows(m)], self.p.X
        if d == 1:
            return self.to_slot(0, hop, 1, m, X), self.to_slot(3, hop, 2, m, X + 1)
        return (self.to_slot(0, hop, 2, m, X - 1),)

    def forward_copy(self, m):
        return self.to_slot(0, self.slot(1, m), 2, m, 1)

    def shift_do(self, own, what, sends=None):
        p = self.p
        sends = self.sends if sends is None else sends
        last = p.X - 1

        def act(copy):
            if what == "start":
                copy.start()
            else:
                copy.wait_send()

        for d in (1, 2):

            @pl.when(p.x >= d)
            def _():
                for m in sends:
                    act(self.direct(own, d, m))

            @pl.when((p.yh >= 1) & (p.x == d - 1))
            def _():
                for m in sends:
                    if m in self.detour:
                        act(self.aside(own, d, m, last if d == 1 else 1))
                for m in sends:
                    if m not in self.detour:
                        act(self.direct(own, d, m))

    def shift_send(self, own, sends=None):
        self.shift_do(own, "start", sends)

    def shift_drain(self, own):
        p = self.p
        last = p.X - 1
        self.shift_do(own, "wait")
        for d in (1, 2):

            @pl.when((p.yh >= 1) & (p.x == p.X - d))
            def _():
                for m in self.detour:
                    for copy in self.relay_copies(d, m):
                        copy.wait_send()

        @pl.when((p.yh < p.YH - 1) & (p.x == last))
        def _():
            for m in self.sends:
                if m not in self.detour:
                    self.forward_copy(m).wait_send()

    def relay(self):
        p = self.p
        for d in (1, 2):

            @pl.when((p.yh >= 1) & (p.x == p.X - d))
            def _():
                for m in self.detour:
                    there = self.hop.at[self.rows(m)]
                    remote(there, there, self.sh_s.at[0, m], self.sh_r.at[0, m], {"video": p.v - 1}).wait_recv()
                    for copy in self.relay_copies(d, m):
                        copy.start()

    def got(self, d, m):
        there = self.slot(d, m)
        remote(there, there, self.sh_s.at[d, m], self.sh_r.at[d, m], {"video": self.p.v - 1}).wait_recv()

    def forward(self):
        p = self.p

        @pl.when((p.yh < p.YH - 1) & (p.x == p.X - 1))
        def _():
            for m in self.sends:
                if m not in self.detour:
                    self.got(1, m)
                    self.forward_copy(m).start()

    def shift_wait(self, sends):
        p = self.p

        @pl.when(p.x < p.X - 1)
        def _():
            for m in sends:
                self.got(1, m)

        @pl.when((p.yh < p.YH - 1) & (p.x == p.X - 1))
        def _():
            for m in sends:
                if m in self.detour:
                    self.got(1, m)

        @pl.when(p.v < p.V - 2)
        def _():
            for m in sends:
                self.got(2, m)

    def messages(self, chunk):
        per = PARTS // self.chunks
        return [chunk * per + i for i in range(per)]

    def pre_grad(self, chunks):
        w, step = self.w, self.step
        def fn(at):
            rows = slice(at, at + step)
            gact = jnp.dot(self.gcat[rows, :], self.wt[...], preferred_element_type=F32)
            gpre = gact.astype(BF16).astype(F32) * self.slope[rows, :]
            self.pad[at + self.cols : at + self.cols + step, w : 2 * w] = gpre.astype(BF16)
            self.spread(at + self.cols, step, gpre)

        for i in chunks:
            self.shift_wait(self.messages(i))
            fn(i * step)

    def edge(self, up, own, at, dst, send, recv):
        cols, px = self.cols, self.px
        if up:
            return remote(own.at[at : at + cols], dst.at[px + cols : px + 2 * cols], send.at[0], recv.at[0], {"section": self.p.s - 1})
        return remote(own.at[at + px - cols : at + px], dst.at[:cols], send.at[1], recv.at[1], {"section": self.p.s + 1})

    def edges(self, what, own, at, dst, send, recv):
        p = self.p

        @pl.when(p.s > 0)
        def _():
            if what == "start":
                self.edge(True, own, at, dst, send, recv).start()
            elif what == "recv":
                self.edge(False, own, at, dst, send, recv).wait_recv()
            else:
                self.edge(True, own, at, dst, send, recv).wait_send()

        @pl.when(p.s < p.S - 1)
        def _():
            if what == "start":
                self.edge(False, own, at, dst, send, recv).start()
            elif what == "recv":
                self.edge(True, own, at, dst, send, recv).wait_recv()
            else:
                self.edge(False, own, at, dst, send, recv).wait_send()

    def halo(self, what):
        mid = self.pad.at[:, self.w : 2 * self.w]
        self.edges(what, mid, self.cols, mid, self.ha_s, self.ha_r)
        if what == "recv":
            for at in (0, self.px + self.cols):
                self.spread(at, self.cols, self.pad[at : at + self.cols, self.w : 2 * self.w].astype(F32))

    def spread(self, at, rows, gpre):
        w = self.w
        col = lax.rem(lax.broadcasted_iota(jnp.int32, (rows, w), 0), self.cols)
        to = slice(at, at + rows)
        self.pad[to, :w] = jnp.where(col == self.cols - 1, 0.0, pltpu.roll(gpre, rows - 1, 0)).astype(BF16)
        self.pad[to, 2 * w :] = jnp.where(col == 0, 0.0, pltpu.roll(gpre, 1, 0)).astype(BF16)

    def src_halo(self, what, own):
        self.edges(what, own, 0, self.src, self.in_s, self.in_r)

    def turn_src(self):
        for ky in range(3):
            self.src_t[ky] = self.src[ky * self.cols : ky * self.cols + self.px, :].T
        self.act_t[...] = self.act[...].T

    def grad_in(self, out, lanes, chunks):
        w, step = self.w, self.step

        def fn(at):
            rows = pl.ds(at, step)
            total = self.gcat[rows, 2 * w :].astype(F32)
            for ky in range(3):
                x = self.pad[pl.ds(at + (2 - ky) * self.cols, step), :]
                total = total + jnp.dot(x, self.wc[ky * 3 * w : (ky + 1) * 3 * w, :], preferred_element_type=F32)
            out[rows, lanes] = total.astype(BF16)

        self.each(fn, chunks)

    def put(self, part, k, grad):
        w = self.w
        q = part.shape[1]
        rows = jnp.concatenate([grad[:, i * w : (i + 1) * w] for i in range(3)], axis=0)
        n = 3 * w // q
        part[k * n : (k + 1) * n] = rows.reshape(n, q, w)

    def products(self, k, lo, hi):
        if k == 3:
            return jnp.dot(self.act_t[:, lo:hi], self.gcat[lo:hi, :], preferred_element_type=F32)
        return jnp.dot(self.src_t[k, :, lo:hi], self.pad[self.cols + lo : self.cols + hi, :], preferred_element_type=F32)

    def grads_early(self, kinds):
        lo, hi = self.order[-1] * self.step, (self.order[-1] + 1) * self.step
        for k in kinds:
            self.early[k] = self.products(k, 0, lo) + self.products(k, hi, self.px)

    def grads_late(self, part, kinds):
        lo, hi = self.order[-1] * self.step, (self.order[-1] + 1) * self.step
        for k in kinds:
            self.put(part, k, self.early[k] + self.products(k, lo, hi))

    def grads(self, part, kinds):
        for k in kinds:
            self.put(part, k, self.products(k, 0, self.px))


def kernel(sizes, cols, scale, *refs):
    g, in1, pre1, in2, pre2, s1, t1, s2, t2 = refs[:9]
    gin, out1, out2 = refs[9:12]
    refs = refs[12:]
    two_refs, refs = refs[:20], refs[20:]
    one_refs, refs = refs[:20], refs[20:]
    r2_refs, refs = refs[:8] + (out2,) + refs[8:22], refs[22:]
    r1_refs, refs = refs[:8] + (out1,) + refs[8:22], refs[22:]
    (ld,) = refs

    p = Place(sizes)
    two = Block(p, cols, (0, 3, 1, 2), DETOUR_TWO, two_refs)
    one = Block(p, cols, (0, 3, 2, 1), DETOUR_ONE, one_refs)
    red2 = Reduce(p, ("y", "x", "z"), scale, r2_refs)
    red1 = Reduce(p, ("x", "z", "y"), scale, r1_refs)
    w = two.w

    barrier = pltpu.get_barrier_semaphore()
    partners = [p.mate()]
    for axis in ("x", "y", "z"):
        partners += [p.peer(axis, lax.rem(p.at[axis] + off, p.n[axis])) for off in far(p.n[axis])]
    partners += [{"video": lax.rem(p.v + off, p.V)} for off in (1, 2, 3, p.V - 3, p.V - 2, p.V - 1)]
    for to in partners:
        pl.semaphore_signal(barrier, inc=1, device_id=to, device_id_type=MESH)

    own2 = two.gcat.at[:, 2 * w :]
    own1 = one.gcat.at[:, 2 * w :]
    body = slice(cols, cols + two.px)
    loads = [(pre2, two.pre), (t2, two.tw), (g, own2), (s2, two.sw), (in2, two.src.at[body]),
             (pre1, one.pre), (t1, one.tw), (s1, one.sw), (in1, one.src.at[body])]
    loads = [pltpu.make_async_copy(a, b, ld.at[i]) for i, (a, b) in enumerate(loads)]
    for c in loads:
        c.start()
    two.clear_edges()
    one.clear_edges()
    pl.semaphore_wait(barrier, len(partners))

    two.shift_send(g)
    two.src_halo("start", in2)
    one.src_halo("start", in1)
    for c in loads:
        c.wait()
    two.activate()
    two.turn_weights()
    two.relay()
    one.activate()
    one.turn_weights()
    two.src_halo("recv", in2)
    one.src_halo("recv", in1)
    two.turn_src()
    two.forward()
    two.pre_grad((0, 3))
    two.halo("start")
    two.pre_grad((1, 2))
    for chunk in (1, 2):
        two.grad_in(one.gcat, slice(2 * w, 3 * w), (chunk,))
        one.shift_send(own1, one.messages(chunk))
    two.halo("recv")
    for chunk in (0, 3):
        two.grad_in(one.gcat, slice(2 * w, 3 * w), (chunk,))
        one.shift_send(own1, one.messages(chunk))
    two.grads(red2.part, (3, 0, 1, 2))
    red2.core_send()
    one.turn_src()
    red2.a_send()
    one.relay()
    one.forward()
    one.pre_grad((0, 3))
    one.halo("start")
    one.pre_grad((2,))
    one.grads_early((3, 0, 1, 2))
    one.pre_grad((1,))
    for k in (3, 0, 2, 1):
        one.grads_late(red1.part, (k,))
        red1.core_send_part(k)
    one.grad_in(gin, slice(0, w), (1, 2))
    red2.b_send()
    red1.a_send()
    one.halo("recv")
    one.grad_in(gin, slice(0, w), (0, 3))
    red2.c_send()
    red1.b_send()
    red2.gb_send()
    red1.c_send()
    red2.ga_send()
    red1.gb_send()
    red1.ga_send()
    red2.core_gather()
    red1.core_gather()
    red2.finish()
    red1.finish()
    two.shift_drain(g)
    one.shift_drain(own1)
    two.halo("drain")
    one.halo("drain")
    two.src_halo("drain", in2)
    one.src_halo("drain", in1)
    red2.drain()
    red1.drain()


def store_kernel(gin, out1, out2, gin_to, gs1_to, gt1_to, gs2_to, gt2_to, wide1, wide2, sem):
    copies = [pltpu.make_async_copy(gin, gin_to, sem.at[0])]
    copies[0].start()
    for k, (src, wide, s_to, t_to) in enumerate(((out1, wide1, gs1_to, gt1_to), (out2, wide2, gs2_to, gt2_to))):
        wide[...] = src[...].astype(F32)
        n = s_to.shape[0]
        for i, (a, b) in enumerate(((wide.at[:n], s_to), (wide.at[n:], t_to))):
            c = pltpu.make_async_copy(a, b, sem.at[1 + 2 * k + i])
            c.start()
            copies.append(c)
    for c in copies:
        c.wait()


def block_scratch(px, cols, w):
    dma = pltpu.SemaphoreType.DMA((2,))
    many = pltpu.SemaphoreType.DMA((4, PARTS))
    return [
        pltpu.VMEM((px + 2 * cols, w), BF16),
        pltpu.VMEM((px, w), BF16),
        pltpu.VMEM((3, 3, w, w), BF16),
        pltpu.VMEM((3, w, w), BF16),
        pltpu.VMEM((px, 3 * w), BF16),
        pltpu.VMEM((px + 2 * cols, 3 * w), BF16),
        pltpu.VMEM((px, w), BF16),
        pltpu.VMEM((px, w), F32),
        pltpu.VMEM((9 * w, w), BF16),
        pltpu.VMEM((3 * w, w), BF16),
        pltpu.VMEM((px, w), BF16),
        pltpu.VMEM((3, w, px), BF16),
        pltpu.VMEM((w, px), BF16),
        pltpu.VMEM((4, w, 3 * w), F32),
        many, many, dma, dma, dma, dma,
    ]


def on_device(sizes, grad_latent, input_one, preact_one, input_two, preact_two,
              spatial_one, temporal_one, spatial_two, temporal_two):
    shape = grad_latent.shape
    rows, cols, w = shape[2:]
    px = rows * cols
    S, V, D = sizes
    scale = 1.0 / math.sqrt(D * V * S * px)
    X = min(XS, V)
    n = {"x": X, "y": V // X * S, "z": D // CORES}
    order1, order2 = ("x", "z", "y"), ("y", "x", "z")
    v1, k1 = reduce_scratch(n, order1, w)
    v2, k2 = reduce_scratch(n, order2, w)
    stay = lambda a: pltpu.with_memory_space_constraint(a, pltpu.HBM)
    flat = lambda a: stay(a.reshape(px, w))
    hbm = pl.BlockSpec(memory_space=pl.ANY)
    vmem = pl.BlockSpec(memory_space=pltpu.VMEM)
    sums = [jax.ShapeDtypeStruct((CORES * v[3].shape[0],) + v[3].shape[1:], WIRE) for v in (v1, v2)]
    gin, out1, out2 = pl.pallas_call(
        functools.partial(kernel, sizes, cols, scale),
        out_shape=(jax.ShapeDtypeStruct((px, w), BF16), *sums),
        in_specs=[pl.BlockSpec(memory_space=pltpu.HBM)] * 9,
        out_specs=[vmem] * 3,
        scratch_shapes=block_scratch(px, cols, w) + block_scratch(px, cols, w)
        + v2 + k2 + v1 + k1 + [pltpu.SemaphoreType.DMA((9,))],
        compiler_params=pltpu.CompilerParams(
            collective_id=0, has_side_effects=True, vmem_limit_bytes=LIMIT
        ),
    )(flat(grad_latent), flat(input_one), flat(preact_one), flat(input_two), flat(preact_two),
      stay(spatial_one), stay(temporal_one), stay(spatial_two), stay(temporal_two))
    tile = lambda a: a.reshape((a.shape[0] * a.shape[1],) + a.shape[2:])
    out1, out2 = tile(out1), tile(out2)
    f32 = lambda a, tiles: jax.ShapeDtypeStruct((tiles * w // a.shape[1],) + a.shape[1:], F32)
    gin, gs1, gt1, gs2, gt2 = pl.pallas_call(
        store_kernel,
        out_shape=(jax.ShapeDtypeStruct((px, w), BF16), f32(out1, 9), f32(out1, 3), f32(out2, 9), f32(out2, 3)),
        in_specs=[vmem] * 3,
        out_specs=[hbm] * 5,
        scratch_shapes=[pltpu.VMEM(out1.shape, F32), pltpu.VMEM(out2.shape, F32), pltpu.SemaphoreType.DMA((5,))],
        compiler_params=pltpu.CompilerParams(vmem_limit_bytes=8 * 1024 * 1024),
    )(gin, out1, out2)
    ss, ts = spatial_one.shape, temporal_one.shape
    return gin.reshape(shape), gs1.reshape(ss), gt1.reshape(ts), gs2.reshape(ss), gt2.reshape(ts)


def solution(mesh):
    sizes = tuple(mesh.shape[k] for k in ("section", "video", "dp"))
    spec = P("dp", "video", "section", None, None)
    return jax.shard_map(
        functools.partial(on_device, sizes),
        mesh=mesh,
        in_specs=(spec,) * 5 + (P(),) * 4,
        out_specs=(spec, P(), P(), P(), P()),
        check_vma=False,
    )
```
